512 devices in a mesh: ctx: 64 (over z, y), ch: 8 (over x, core).
Axes of the slice: x: 4, y: 4, z: 16, core: 2. Of those that a mesh axis runs over, the one named last changes fastest.
Arguments:
- query_proj: bfloat16 [16384, 1024], P('ctx', 'ch'), may hold values from -16 to 16
- key_proj: bfloat16 [16384, 1024], P('ctx', 'ch'), may hold values from -8 to 8
- value_proj: bfloat16 [16384, 1024], P('ctx', 'ch'), may hold values from 0.25 to 1.75
- decays: float32 [1024, 16], replicated, may hold values from 1.2207031e-05 to 0.1, as said below
- residues: float32 [1024, 16], replicated, may hold values from -1.5 to 1.5
- skip_gain: float32 [1024], P('ch'), may hold values from -6 to 6
Outputs:
- mixed: bfloat16 [16384, 1024], P('ctx', 'ch')
The draws below stay inside these ranges and needn't reach their ends.
Inputs may be any that keep to these rules, and one draw needn't show every extreme that they name: `decays`: every rate is positive and no larger than 0.1; each channel has at least one mode slower than 2 / 16384 and one faster.
All inputs are finite; a program needn't handle non-finite values.
Results may differ from the reference program's by a relative error of at most 0.0042.
Values may be sent and summed in bfloat16 or wider, within the bound.
A program may use at most 64 MiB of HBM per device.

```python
import math
import jax
import jax.numpy as jnp
from jax import lax

ORDER = 16
CHANNELS = 1024
TOKENS = 16384


def segment_loud(key):
    mask_key = jax.random.fold_in(key, 7001)
    segment_total = TOKENS // 256
    picks = jax.random.randint(mask_key, (segment_total, CHANNELS), 0, 20, dtype=jnp.int32)
    return jnp.repeat(picks < 7, 256, axis=0)


def random_signs(key, shape):
    coins = jax.random.randint(key, shape, 0, 2, dtype=jnp.int32)
    return jnp.where(coins == 0, -1.0, 1.0).astype(jnp.float32)


def normal_noise(key, shape):
    return jnp.clip(jax.random.normal(key, shape, jnp.float32), -4.0, 4.0)


def draw_key_proj(key, part):
    loud = segment_loud(key)
    split_keys = jax.random.split(jax.random.fold_in(key, 303), 5)
    shape = (TOKENS, CHANNELS)
    positions = jnp.arange(TOKENS, dtype=jnp.int32)
    within = ((positions % 256).astype(jnp.float32) - 127.5) / 128.0
    cubic = 0.5 * (5.0 * within * within * within - 3.0 * within)
    ramp = ((positions % 64).astype(jnp.float32) - 31.5) / 32.0
    least_amplitude = 1.0
    quiet_level = 0.1
    noise = normal_noise(split_keys[4], shape)
    cubic_weight = jax.random.uniform(split_keys[0], (CHANNELS,), jnp.float32, least_amplitude, 2.0)
    cubic_weight = cubic_weight * random_signs(split_keys[1], (CHANNELS,))
    ramp_weight = jax.random.uniform(split_keys[2], (CHANNELS,), jnp.float32, least_amplitude, 2.0)
    ramp_weight = ramp_weight * random_signs(split_keys[3], (CHANNELS,))
    pattern = cubic[:, None] * cubic_weight[None, :] + ramp[:, None] * ramp_weight[None, :]
    level = jnp.where(loud, 1.0, quiet_level)
    return (level * (pattern + noise)).astype(jnp.bfloat16)


def draw_query_proj(key, part):
    loud = segment_loud(key)
    noise_key = jax.random.fold_in(key, 404)
    shape = (TOKENS, CHANNELS)
    noise = normal_noise(noise_key, shape)
    return (noise * jnp.where(loud, 1.0, 4.0)).astype(jnp.bfloat16)


def draw_residues(key, part):
    first_key, second_key, third_key = jax.random.split(jax.random.fold_in(key, 202), 3)
    shape = (CHANNELS, ORDER)
    base = jnp.clip(0.25 * jax.random.normal(first_key, shape, jnp.float32), -1.5, 1.5)
    band_size = jax.random.uniform(second_key, shape, jnp.float32, 0.6, 1.2)
    band_sign = random_signs(third_key, (CHANNELS, 1))
    mode_ids = jnp.arange(ORDER, dtype=jnp.int32)[None, :]
    in_band = jnp.logical_or(mode_ids == 1, mode_ids == 2)
    return jnp.where(in_band, band_sign * band_size, base).astype(jnp.float32)


def draw_decays(key, part):
    first_key, second_key, third_key, fourth_key = jax.random.split(jax.random.fold_in(key, 101), 4)
    shape = (CHANNELS, ORDER)
    length = float(TOKENS)
    share = 0.5
    slow_log = jax.random.uniform(first_key, shape, jnp.float32, math.log(0.2 / length), math.log(2.0 / length))
    fast_log = jax.random.uniform(second_key, shape, jnp.float32, math.log(2.0 / length), math.log(0.1))
    band_log = jax.random.uniform(fourth_key, shape, jnp.float32, math.log(1.0 / 256.0), math.log(1.0 / 64.0))
    picked = jax.random.uniform(third_key, shape, jnp.float32) < share
    mode_ids = jnp.arange(ORDER, dtype=jnp.int32)[None, :]
    chosen_log = jnp.where(picked, slow_log, fast_log)
    chosen_log = jnp.where(mode_ids == 0, slow_log, chosen_log)
    chosen_log = jnp.where(jnp.logical_or(mode_ids == 1, mode_ids == 2), band_log, chosen_log)
    return jnp.exp(chosen_log).astype(jnp.float32)


def levels(own_key, dims, cuts, least, high):
    factor_of, own = 1.0, jax.random.fold_in(own_key, 6)
    for axis_at, parts in cuts:
        heights = jnp.exp(jax.random.uniform(jax.random.fold_in(own, axis_at), (parts,), jnp.float32, least / len(cuts), high / len(cuts)))
        factor_of = factor_of * jnp.repeat(heights, dims[axis_at] // parts).reshape([-1 if axis == axis_at else 1 for axis in range(len(dims))])
    return factor_of


def normal_values(own_key, dims, scale, reach, shards=(), kind=jnp.bfloat16):
    gain = levels(own_key, dims, shards, -0.22, 0.18) if shards else 1.0
    result = jax.random.normal(own_key, dims, jnp.float32) * scale * gain
    return jnp.minimum(jnp.maximum(result, -reach), reach).astype(kind)


def setup_inputs(seed: int = 0) -> dict:
    splits = jax.random.split(jax.random.key(seed), 7)
    return {
        "query_proj": draw_query_proj(jax.random.fold_in(splits[6], 71), 0),
        "key_proj": draw_key_proj(jax.random.fold_in(splits[6], 71), 0),
        "value_proj": jnp.clip(0.25 + 1.5 * jax.random.uniform(splits[2], (TOKENS, CHANNELS), jnp.float32) ** levels(splits[2], (TOKENS, CHANNELS), ((0, 64), (1, 8)), -0.2, 0.2), 0.25, 1.75).astype(jnp.bfloat16),
        "decays": draw_decays(jax.random.fold_in(splits[6], 71), 0),
        "residues": draw_residues(jax.random.fold_in(splits[6], 71), 0),
        "skip_gain": normal_values(splits[5], (CHANNELS,), 1.0, 6.0, ((0, 8),), jnp.float32),
    }


def reference(query_proj, key_proj, value_proj, decays, residues, skip_gain):
    block_width = 128 if CHANNELS % 128 == 0 else CHANNELS
    block_total = CHANNELS // block_width
    step_ids = jnp.arange(TOKENS, dtype=jnp.int32).astype(jnp.float32)

    def by_block(matrix):
        return matrix.reshape(matrix.shape[0], block_total, block_width).transpose(1, 0, 2)

    def one_block(inputs):
        query_block, key_block, value_block, rate_block, weight_block, gain_block = inputs
        gated_in = (key_block.astype(jnp.float32) * value_block.astype(jnp.float32)).astype(jnp.bfloat16)
        profile = jnp.zeros((TOKENS, block_width), jnp.float32)
        for mode_idx in range(ORDER):
            rate = rate_block[:, mode_idx]
            scale = weight_block[:, mode_idx] * jnp.sqrt(2.0 * rate)
            profile = profile + scale[None, :] * jnp.exp(-rate[None, :] * step_ids[:, None])
        signal = gated_in.astype(jnp.float32)
        spectrum = jnp.fft.rfft(signal, n=2 * TOKENS, axis=0) * jnp.fft.rfft(profile, n=2 * TOKENS, axis=0)
        conv = jnp.fft.irfft(spectrum, n=2 * TOKENS, axis=0)[:TOKENS]
        return (query_block.astype(jnp.float32) * (conv + gain_block[None, :] * signal)).astype(jnp.bfloat16)
    outputs = lax.map(one_block, (by_block(query_proj), by_block(key_proj), by_block(value_proj), decays.reshape(block_total, block_width, ORDER), residues.reshape(block_total, block_width, ORDER), skip_gain.reshape(block_total, block_width)))
    return outputs.transpose(1, 0, 2).reshape(TOKENS, CHANNELS)
```

```python
import jax
import jax.numpy as jnp
from jax import lax
from jax.experimental import pallas as pl
from jax.experimental.pallas import tpu as pltpu
from jax.sharding import PartitionSpec as P

MESH = pl.DeviceIdType.MESH
F32 = jnp.float32
ROWS = 8
Y_COUNT = 4


def far_first(count):
    return sorted(range(1, count), key=lambda step: (-min(step, count - step), step))


def kernel(
    query_hbm, key_hbm, value_hbm, decay_hbm, weight_hbm, gain_hbm, out_hbm,
    query_buf, key_buf, value_buf, decay_buf, weight_buf, gain_buf, out_buf,
    signal, shifted, table, taps, base, near, power, prefix,
    own_state, row_states, row_total, column_states,
    load_sems, store_sem, y_send, y_recv, z_send, z_recv,
):
    row_count, lane_count = query_buf.shape
    mode_count = decay_buf.shape[0]
    block_count = row_count // ROWS
    ctx_count = lax.axis_size("ctx")
    z_count = ctx_count // Y_COUNT
    ctx = lax.axis_index("ctx")
    z_at = ctx // Y_COUNT
    y_at = ctx % Y_COUNT
    lanes = pl.ds(pl.multiple_of(lax.axis_index("ch") * lane_count, lane_count), lane_count)

    loads = [
        pltpu.make_async_copy(source, target, load_sems.at[slot])
        for slot, (source, target) in enumerate(
            [
                (decay_hbm.at[:, lanes], decay_buf),
                (key_hbm, key_buf),
                (value_hbm, value_buf),
                (weight_hbm.at[:, lanes], weight_buf),
                (gain_hbm, gain_buf),
                (query_hbm, query_buf),
            ]
        )
    ]
    for load in loads:
        load.start()

    barrier = pltpu.get_barrier_semaphore()
    for step in range(1, Y_COUNT):
        peer = z_at * Y_COUNT + (y_at + step) % Y_COUNT
        pl.semaphore_signal(barrier, inc=1, device_id={"ctx": peer}, device_id_type=MESH)
    for step in far_first(z_count):

        @pl.when(z_at >= step)
        def _(step=step):
            peer = ctx - step * Y_COUNT
            pl.semaphore_signal(barrier, inc=1, device_id={"ctx": peer}, device_id_type=MESH)

    loads[0].wait()
    decay = decay_buf[...]
    loads[1].wait()
    loads[2].wait()
    product = key_buf[...].astype(F32) * value_buf[...].astype(F32)
    signal[0:64, :] = jnp.zeros((64, lane_count), F32)
    signal[64:, :] = product.astype(jnp.bfloat16).astype(F32)
    sub = lax.broadcasted_iota(jnp.int32, (ROWS, lane_count), 0).astype(F32)
    rate = [jnp.broadcast_to(decay_buf[r : r + 1, :], (ROWS, lane_count)) for r in range(mode_count)]
    leap = [jnp.exp(-float(ROWS) * rate[r]) for r in range(mode_count)]

    def gather(block, sums):
        rows = signal[pl.ds(pl.multiple_of(64 + ROWS * block, ROWS), ROWS), :]
        return tuple(leap[r] * sums[r] + rows for r in range(mode_count))

    sums = lax.fori_loop(
        0, block_count, gather, (jnp.zeros((ROWS, lane_count), F32),) * mode_count, unroll=4
    )
    for r in range(mode_count):
        fade = jnp.exp(-rate[r] * (float(ROWS - 1) - sub))
        own_state[r : r + 1, :] = jnp.sum(sums[r] * fade, axis=0, keepdims=True)

    pl.semaphore_wait(barrier, Y_COUNT - 1 + (z_count - 1 - z_at))

    y_copies = []
    for step in range(1, Y_COUNT):
        peer_y = (y_at + step) % Y_COUNT
        copy = pltpu.make_async_remote_copy(
            src_ref=own_state,
            dst_ref=row_states.at[step],
            send_sem=y_send.at[step],
            recv_sem=y_recv.at[step],
            device_id={"ctx": z_at * Y_COUNT + peer_y},
            device_id_type=MESH,
        )
        copy.start()
        y_copies.append(copy)
    span = float(row_count)
    for step in range(1, z_count):
        power[step] = jnp.exp(decay * (-span * Y_COUNT * (step - 1)))
    y_f = y_at.astype(F32)
    for copy in y_copies:
        copy.wait_recv()
    total = own_state[...] * jnp.exp(decay * (-span * (Y_COUNT - 1 - y_f)))
    before = jnp.zeros_like(decay)
    for step in range(1, Y_COUNT):
        source = (y_at - step + Y_COUNT) % Y_COUNT
        state = row_states[step]
        total = total + state * jnp.exp(decay * (-span * (Y_COUNT - 1 - source.astype(F32))))
        ahead = jnp.maximum(y_at - 1 - source, 0).astype(F32)
        seen = jnp.where(source < y_at, 1.0, 0.0)
        before = before + state * (seen * jnp.exp(decay * (-span * ahead)))
    row_total[...] = total
    prefix[...] = before

    def z_copy(step):
        return pltpu.make_async_remote_copy(
            src_ref=row_total,
            dst_ref=column_states.at[step],
            send_sem=z_send.at[step],
            recv_sem=z_recv.at[step],
            device_id={"ctx": lax.rem(ctx + step * Y_COUNT, ctx_count)},
            device_id_type=MESH,
        )

    for step in far_first(z_count):

        @pl.when(z_at + step < z_count)
        def _(step=step):
            z_copy(step).start()

    loads[3].wait()
    loads[4].wait()
    weight = weight_buf[...] * jnp.sqrt(2.0 * decay)
    weight_buf[...] = weight
    start = tuple(weight_buf[r : r + 1, :] * jnp.exp(-rate[r] * sub) for r in range(mode_count))

    def tabulate(block, modes):
        total = modes[0]
        for r in range(1, mode_count):
            total = total + modes[r]
        taps[pl.ds(pl.multiple_of(ROWS * block, ROWS), ROWS), :] = total
        for r in range(mode_count):
            table[block, r] = modes[r]
        return tuple(modes[r] * leap[r] for r in range(mode_count))

    lax.fori_loop(0, block_count, tabulate, start)

    for shift in range(ROWS):
        shifted[shift, 0:56, :] = jnp.zeros((56, lane_count), F32)
        shifted[shift, 56:, :] = signal[64 - shift : 64 + row_count - shift, :]
    gain = gain_buf[...]
    for group in range(row_count // 64):

        def slide(lag, sums, group=group):
            for shift in range(ROWS):
                tap = taps[pl.ds(lag * ROWS + shift, 1), :]
                rows = shifted[shift, pl.ds(pl.multiple_of(64 * group + 56 - ROWS * lag, ROWS), 64), :]
                sums = sums + tap * rows
            return sums

        rows = slice(64 * group, 64 * group + 64)
        first = gain * signal[64 + 64 * group : 128 + 64 * group, :]
        base[rows, :] = lax.fori_loop(0, 8 * group + 8, slide, first)
    loads[5].wait()

    near[...] = jnp.zeros_like(decay)
    for step in range(1, z_count):

        @pl.when(z_at >= step)
        def _(step=step):
            z_copy(step).wait_recv()
            near[...] += power[step] * column_states[step]

    entering = prefix[...] + near[...] * jnp.exp(decay * (-span * y_f))
    near[...] = entering * jnp.exp(-decay)
    modes = [jnp.broadcast_to(near[r : r + 1, :], (ROWS, lane_count)) for r in range(mode_count)]

    def finish(pair, carry):
        tiles = []
        for half in range(2):
            block = 2 * pair + half
            total = base[pl.ds(pl.multiple_of(ROWS * block, ROWS), ROWS), :]
            for r in range(mode_count):
                total = total + table[block, r] * modes[r]
            tiles.append(total)
        rows = pl.ds(pl.multiple_of(2 * ROWS * pair, 2 * ROWS), 2 * ROWS)
        mixed = query_buf[rows, :].astype(F32) * jnp.concatenate(tiles, axis=0)
        out_buf[rows, :] = mixed.astype(jnp.bfloat16)
        return carry

    lax.fori_loop(0, block_count // 2, finish, 0)
    store = pltpu.make_async_copy(out_buf, out_hbm, store_sem)
    store.start()
    for copy in y_copies:
        copy.wait_send()
    for step in range(1, z_count):

        @pl.when(z_at + step < z_count)
        def _(step=step):
            z_copy(step).wait_send()

    store.wait()


def local(query_proj, key_proj, value_proj, decays, residues, skip_gain):
    row_count, lane_count = query_proj.shape
    mode_count = decays.shape[1]
    ctx_count = lax.axis_size("ctx")
    z_count = ctx_count // Y_COUNT
    state = (mode_count, lane_count)
    wide = (row_count, lane_count)
    block_count = row_count // ROWS
    any_space = pl.BlockSpec(memory_space=pl.ANY)
    return pl.pallas_call(
        kernel,
        out_shape=jax.ShapeDtypeStruct(wide, jnp.bfloat16),
        in_specs=[any_space] * 6,
        out_specs=any_space,
        scratch_shapes=[
            pltpu.VMEM(wide, jnp.bfloat16),
            pltpu.VMEM(wide, jnp.bfloat16),
            pltpu.VMEM(wide, jnp.bfloat16),
            pltpu.VMEM(state, F32),
            pltpu.VMEM(state, F32),
            pltpu.VMEM((1, lane_count), F32),
            pltpu.VMEM(wide, jnp.bfloat16),
            pltpu.VMEM((64 + row_count, lane_count), F32),
            pltpu.VMEM((ROWS, 56 + row_count, lane_count), F32),
            pltpu.VMEM((block_count, mode_count, ROWS, lane_count), F32),
            pltpu.VMEM(wide, F32),
            pltpu.VMEM(wide, F32),
            pltpu.VMEM(state, F32),
            pltpu.VMEM((z_count,) + state, F32),
            pltpu.VMEM(state, F32),
            pltpu.VMEM(state, F32),
            pltpu.VMEM((Y_COUNT,) + state, F32),
            pltpu.VMEM(state, F32),
            pltpu.VMEM((z_count,) + state, F32),
            pltpu.SemaphoreType.DMA((6,)),
            pltpu.SemaphoreType.DMA,
            pltpu.SemaphoreType.DMA((Y_COUNT,)),
            pltpu.SemaphoreType.DMA((Y_COUNT,)),
            pltpu.SemaphoreType.DMA((z_count,)),
            pltpu.SemaphoreType.DMA((z_count,)),
        ],
        compiler_params=pltpu.CompilerParams(collective_id=0, has_side_effects=True),
    )(query_proj, key_proj, value_proj, decays.T, residues.T, skip_gain.reshape(1, lane_count))


def solution(mesh):
    return jax.shard_map(
        local,
        mesh=mesh,
        in_specs=(P("ctx", "ch"), P("ctx", "ch"), P("ctx", "ch"), P(), P(), P("ch")),
        out_specs=P("ctx", "ch"),
        check_vma=False,
    )
```

```python
import jax
import jax.numpy as jnp
from jax import lax
from jax.experimental import pallas as pl
from jax.experimental.pallas import tpu as pltpu
from jax.sharding import PartitionSpec as P

MESH = pl.DeviceIdType.MESH
F32 = jnp.float32
ROWS = 8
Y_COUNT = 4
FIRST_END = 4
SECOND_END = 7
HUB = 10


def last_target(z_at, z_count):
    return jnp.where(z_at < FIRST_END - 1, FIRST_END - 1, jnp.where(z_at < SECOND_END - 1, SECOND_END - 1, z_count - 1))


def first_source(z_at):
    return jnp.where(z_at < FIRST_END, 0, jnp.where(z_at < SECOND_END, FIRST_END - 1, SECOND_END - 1))


def far_first(count):
    return sorted(range(1, count), key=lambda step: (-min(step, count - step), step))


def kernel(
    query_hbm, key_hbm, value_hbm, decay_hbm, weight_hbm, gain_hbm, out_hbm,
    query_buf, key_buf, value_buf, decay_buf, weight_buf, gain_buf, out_buf,
    signal, shifted, table, taps, base, near, power, prefix,
    own_state, row_states, row_total, column_states,
    load_sems, store_sem, y_send, y_recv, z_send, z_recv, ready, go,
):
    row_count, lane_count = query_buf.shape
    mode_count = decay_buf.shape[0]
    block_count = row_count // ROWS
    ctx_count = lax.axis_size("ctx")
    z_count = ctx_count // Y_COUNT
    ctx = lax.axis_index("ctx")
    z_at = ctx // Y_COUNT
    y_at = ctx % Y_COUNT
    lanes = pl.ds(pl.multiple_of(lax.axis_index("ch") * lane_count, lane_count), lane_count)

    loads = [
        pltpu.make_async_copy(source, target, load_sems.at[slot])
        for slot, (source, target) in enumerate(
            [
                (decay_hbm.at[:, lanes], decay_buf),
                (key_hbm, key_buf),
                (value_hbm, value_buf),
                (weight_hbm.at[:, lanes], weight_buf),
                (gain_hbm, gain_buf),
                (query_hbm, query_buf),
            ]
        )
    ]
    for load in loads:
        load.start()

    barrier = pltpu.get_barrier_semaphore()
    target_end = last_target(z_at, z_count)
    source_start = first_source(z_at)
    early_sender = z_at < SECOND_END - 1
    early_target = z_at < SECOND_END
    late_member = jnp.logical_and(z_at >= SECOND_END - 1, z_at != HUB)
    forwards = jnp.logical_or(z_at == FIRST_END - 1, z_at == SECOND_END - 1)

    def tell(semaphore, peer):
        pl.semaphore_signal(semaphore, inc=1, device_id={"ctx": peer}, device_id_type=MESH)

    for step in range(1, Y_COUNT):
        tell(barrier, z_at * Y_COUNT + (y_at + step) % Y_COUNT)
    for step in range(1, FIRST_END):

        @pl.when(jnp.logical_and(early_sender, z_at + step <= target_end))
        def _(step=step):
            tell(barrier, ctx + step * Y_COUNT)

    @pl.when(late_member)
    def _():
        tell(barrier, HUB * Y_COUNT + y_at)

    loads[0].wait()
    decay = decay_buf[...]
    loads[1].wait()
    loads[2].wait()
    product = key_buf[...].astype(F32) * value_buf[...].astype(F32)
    signal[0:64, :] = jnp.zeros((64, lane_count), F32)
    signal[64:, :] = product.astype(jnp.bfloat16).astype(F32)
    sub = lax.broadcasted_iota(jnp.int32, (ROWS, lane_count), 0).astype(F32)
    rate = [jnp.broadcast_to(decay_buf[r : r + 1, :], (ROWS, lane_count)) for r in range(mode_count)]
    leap = [jnp.exp(-float(ROWS) * rate[r]) for r in range(mode_count)]

    def gather(block, sums):
        rows = signal[pl.ds(pl.multiple_of(64 + ROWS * block, ROWS), ROWS), :]
        return tuple(leap[r] * sums[r] + rows for r in range(mode_count))

    sums = lax.fori_loop(
        0, block_count, gather, (jnp.zeros((ROWS, lane_count), F32),) * mode_count, unroll=4
    )
    for r in range(mode_count):
        fade = jnp.exp(-rate[r] * (float(ROWS - 1) - sub))
        own_state[r : r + 1, :] = jnp.sum(sums[r] * fade, axis=0, keepdims=True)

    greeted = jnp.where(early_target, z_at - source_start, 0)
    greeted = jnp.where(z_at == HUB, z_count - SECOND_END, greeted)
    pl.semaphore_wait(barrier, Y_COUNT - 1 + greeted)

    for step in range(1, FIRST_END):

        @pl.when(jnp.logical_and(early_target, z_at - step >= source_start))
        def _(step=step):
            tell(ready.at[step], ctx - step * Y_COUNT)

    @pl.when(z_at == HUB)
    def _():
        for row in range(SECOND_END - 1, z_count - 1):
            if row != HUB:
                tell(go, row * Y_COUNT + y_at)

    y_copies = []
    for step in range(1, Y_COUNT):
        peer_y = (y_at + step) % Y_COUNT
        copy = pltpu.make_async_remote_copy(
            src_ref=own_state,
            dst_ref=row_states.at[step],
            send_sem=y_send.at[step],
            recv_sem=y_recv.at[step],
            device_id={"ctx": z_at * Y_COUNT + peer_y},
            device_id_type=MESH,
        )
        copy.start()
        y_copies.append(copy)
    span = float(row_count)
    for step in range(1, z_count):
        power[step] = jnp.exp(decay * (-span * Y_COUNT * (step - 1)))
    loads[3].wait()
    loads[4].wait()
    weight = weight_buf[...] * jnp.sqrt(2.0 * decay)
    weight_buf[...] = weight
    start = tuple(weight_buf[r : r + 1, :] * jnp.exp(-rate[r] * sub) for r in range(mode_count))

    def tabulate(block, modes):
        total = modes[0]
        for r in range(1, mode_count):
            total = total + modes[r]
        taps[pl.ds(pl.multiple_of(ROWS * block, ROWS), ROWS), :] = total
        for r in range(mode_count):
            table[block, r] = modes[r]
        return tuple(modes[r] * leap[r] for r in range(mode_count))

    lax.fori_loop(0, block_count, tabulate, start)

    for shift in range(ROWS):
        shifted[shift, 0:56, :] = jnp.zeros((56, lane_count), F32)
        shifted[shift, 56:, :] = signal[64 - shift : 64 + row_count - shift, :]
    gain = gain_buf[...]
    for group in range(row_count // 64):

        def slide(lag, sums, group=group):
            for shift in range(ROWS):
                tap = taps[pl.ds(lag * ROWS + shift, 1), :]
                rows = shifted[shift, pl.ds(pl.multiple_of(64 * group + 56 - ROWS * lag, ROWS), 64), :]
                sums = sums + tap * rows
            return sums

        rows = slice(64 * group, 64 * group + 64)
        first = gain * signal[64 + 64 * group : 128 + 64 * group, :]
        base[rows, :] = lax.fori_loop(0, 8 * group + 8, slide, first)
    loads[5].wait()

    y_f = y_at.astype(F32)
    for copy in y_copies:
        copy.wait_recv()
    total = own_state[...] * jnp.exp(decay * (-span * (Y_COUNT - 1 - y_f)))
    before = jnp.zeros_like(decay)
    for step in range(1, Y_COUNT):
        source = (y_at - step + Y_COUNT) % Y_COUNT
        state = row_states[step]
        total = total + state * jnp.exp(decay * (-span * (Y_COUNT - 1 - source.astype(F32))))
        ahead = jnp.maximum(y_at - 1 - source, 0).astype(F32)
        seen = jnp.where(source < y_at, 1.0, 0.0)
        before = before + state * (seen * jnp.exp(decay * (-span * ahead)))
    row_total[...] = total
    prefix[...] = before

    def z_copy(step):
        return pltpu.make_async_remote_copy(
            src_ref=row_total,
            dst_ref=column_states.at[step],
            send_sem=z_send.at[step],
            recv_sem=z_recv.at[step],
            device_id={"ctx": lax.rem(ctx + step * Y_COUNT, ctx_count)},
            device_id_type=MESH,
        )

    near[...] = jnp.zeros_like(decay)

    def collect():
        for step in range(1, z_count):

            @pl.when(z_at - step >= source_start)
            def _(step=step):
                z_copy(step).wait_recv()
                near[...] += power[step] * column_states[step]

    @pl.when(forwards)
    def _():
        collect()
        row_total[...] += power[2] * near[...]

    @pl.when(jnp.logical_and(late_member, z_at < z_count - 1))
    def _():
        pl.semaphore_wait(go, 1)

    for step in far_first(z_count):

        @pl.when(z_at + step <= target_end)
        def _(step=step):
            if step < FIRST_END:

                @pl.when(early_sender)
                def _():
                    pl.semaphore_wait(ready.at[step], 1)

            z_copy(step).start()

    @pl.when(jnp.logical_not(forwards))
    def _():
        collect()

    entering = prefix[...] + near[...] * jnp.exp(decay * (-span * y_f))
    near[...] = entering * jnp.exp(-decay)
    modes = [jnp.broadcast_to(near[r : r + 1, :], (ROWS, lane_count)) for r in range(mode_count)]

    def finish(pair, carry):
        tiles = []
        for half in range(2):
            block = 2 * pair + half
            terms = [table[block, r] * modes[r] for r in range(mode_count)]
            terms.append(base[pl.ds(pl.multiple_of(ROWS * block, ROWS), ROWS), :])
            while len(terms) > 1:
                terms = [sum(terms[at : at + 2][1:], terms[at]) for at in range(0, len(terms), 2)]
            tiles.append(terms[0])
        rows = pl.ds(pl.multiple_of(2 * ROWS * pair, 2 * ROWS), 2 * ROWS)
        mixed = query_buf[rows, :].astype(F32) * jnp.concatenate(tiles, axis=0)
        out_buf[rows, :] = mixed.astype(jnp.bfloat16)
        return carry

    lax.fori_loop(0, block_count // 2, finish, 0, unroll=2)
    store = pltpu.make_async_copy(out_buf, out_hbm, store_sem)
    store.start()
    for copy in y_copies:
        copy.wait_send()
    for step in range(1, z_count):

        @pl.when(z_at + step <= target_end)
        def _(step=step):
            z_copy(step).wait_send()

    store.wait()


def local(query_proj, key_proj, value_proj, decays, residues, skip_gain):
    row_count, lane_count = query_proj.shape
    mode_count = decays.shape[1]
    ctx_count = lax.axis_size("ctx")
    z_count = ctx_count // Y_COUNT
    state = (mode_count, lane_count)
    wide = (row_count, lane_count)
    block_count = row_count // ROWS
    any_space = pl.BlockSpec(memory_space=pl.ANY)
    return pl.pallas_call(
        kernel,
        out_shape=jax.ShapeDtypeStruct(wide, jnp.bfloat16),
        in_specs=[any_space] * 6,
        out_specs=any_space,
        scratch_shapes=[
            pltpu.VMEM(wide, jnp.bfloat16),
            pltpu.VMEM(wide, jnp.bfloat16),
            pltpu.VMEM(wide, jnp.bfloat16),
            pltpu.VMEM(state, F32),
            pltpu.VMEM(state, F32),
            pltpu.VMEM((1, lane_count), F32),
            pltpu.VMEM(wide, jnp.bfloat16),
            pltpu.VMEM((64 + row_count, lane_count), F32),
            pltpu.VMEM((ROWS, 56 + row_count, lane_count), F32),
            pltpu.VMEM((block_count, mode_count, ROWS, lane_count), F32),
            pltpu.VMEM(wide, F32),
            pltpu.VMEM(wide, F32),
            pltpu.VMEM(state, F32),
            pltpu.VMEM((z_count,) + state, F32),
            pltpu.VMEM(state, F32),
            pltpu.VMEM(state, F32),
            pltpu.VMEM((Y_COUNT,) + state, F32),
            pltpu.VMEM(state, F32),
            pltpu.VMEM((z_count,) + state, F32),
            pltpu.SemaphoreType.DMA((6,)),
            pltpu.SemaphoreType.DMA,
            pltpu.SemaphoreType.DMA((Y_COUNT,)),
            pltpu.SemaphoreType.DMA((Y_COUNT,)),
            pltpu.SemaphoreType.DMA((z_count,)),
            pltpu.SemaphoreType.DMA((z_count,)),
            pltpu.SemaphoreType.REGULAR((FIRST_END,)),
            pltpu.SemaphoreType.REGULAR,
        ],
        compiler_params=pltpu.CompilerParams(collective_id=0, has_side_effects=True),
    )(query_proj, key_proj, value_proj, decays.T, residues.T, skip_gain.reshape(1, lane_count))


def solution(mesh):
    return jax.shard_map(
        local,
        mesh=mesh,
        in_specs=(P("ctx", "ch"), P("ctx", "ch"), P("ctx", "ch"), P(), P(), P("ch")),
        out_specs=P("ctx", "ch"),
        check_vma=False,
    )
```

```python
import jax
import jax.numpy as jnp
from jax import lax
from jax.experimental import pallas as pl
from jax.experimental.pallas import tpu as pltpu
from jax.sharding import PartitionSpec as P

MESH = pl.DeviceIdType.MESH
F32 = jnp.float32
ROWS = 8
Y_COUNT = 4
FIRST_END = 4
EARLY_END = 7
HUB = 10
NEAR = (1, 2, 3, 4, 5, 6)
FAR = (15, 14, 13, 12, 7, 11)
RELAYED = (8, 11)


def kernel(
    query_hbm, key_hbm, value_hbm, decay_hbm, weight_hbm, gain_hbm, out_hbm,
    query_buf, key_buf, value_buf, decay_buf, weight_buf, gain_buf, out_buf,
    signal, shifted, table, taps, base, near, power, prefix,
    own_state, row_states, row_total, column_states, zero_state,
    load_sems, store_sem, y_send, y_recv, z_send, z_recv, row_ready, ready, go,
    zero_send, zero_recv, zero_ready,
):
    row_count, lane_count = query_buf.shape
    mode_count = decay_buf.shape[0]
    block_count = row_count // ROWS
    ctx_count = lax.axis_size("ctx")
    z_count = ctx_count // Y_COUNT
    ctx = lax.axis_index("ctx")
    z_at = lax.div(ctx, Y_COUNT)
    y_at = ctx - z_at * Y_COUNT
    last = z_count - 1
    early_sender = z_at < EARLY_END - 1
    early_target = z_at < EARLY_END
    apart = lax.axis_index("ch") == 0
    zero = z_at == 0
    target_end = jnp.where(
        z_at < FIRST_END - 1, FIRST_END - 1, jnp.where(early_sender, EARLY_END - 1, last)
    )
    source_start = jnp.where(
        z_at < FIRST_END,
        jnp.where(apart, 1, 0),
        jnp.where(early_target, FIRST_END - 1, EARLY_END - 1),
    )
    send_count = jnp.where(jnp.logical_and(apart, zero), 0, target_end - z_at)
    recv_count = jnp.maximum(z_at - source_start, 0)
    order = jnp.where(jnp.logical_and(apart, zero), lax.rem(y_at + Y_COUNT - 1, Y_COUNT), y_at)
    zero_sender = jnp.logical_and(jnp.logical_and(apart, zero), y_at > 0)
    zero_double = jnp.logical_and(zero_sender, y_at == 1)
    from_zero = jnp.logical_and(apart, z_at > 0)
    direct = jnp.logical_and(from_zero, jnp.logical_or(z_at < RELAYED[0], z_at >= RELAYED[1]))
    relays = jnp.logical_and(apart, z_at == EARLY_END - 1)
    late_member = jnp.logical_and(z_at >= EARLY_END - 1, z_at != HUB)
    forwards = jnp.logical_or(z_at == FIRST_END - 1, z_at == EARLY_END - 1)
    lanes = pl.ds(pl.multiple_of(lax.axis_index("ch") * lane_count, lane_count), lane_count)

    loads = [
        pltpu.make_async_copy(source, target, load_sems.at[slot])
        for slot, (source, target) in enumerate(
            [
                (decay_hbm.at[:, lanes], decay_buf),
                (key_hbm, key_buf),
                (value_hbm, value_buf),
                (weight_hbm.at[:, lanes], weight_buf),
                (gain_hbm, gain_buf),
                (query_hbm, query_buf),
            ]
        )
    ]
    for load in loads:
        load.start()

    barrier = pltpu.get_barrier_semaphore()

    def tell(semaphore, peer):
        pl.semaphore_signal(semaphore, inc=1, device_id={"ctx": peer}, device_id_type=MESH)

    for step in range(1, Y_COUNT):

        @pl.when(order + step < Y_COUNT)
        def _(step=step):
            tell(barrier, z_at * Y_COUNT + lax.rem(y_at + step, Y_COUNT))

    @pl.when(early_sender)
    def _():
        def greet(step, carry):
            tell(barrier, ctx + step * Y_COUNT)
            return carry

        lax.fori_loop(1, send_count + 1, greet, 0)

    @pl.when(zero_sender)
    def _():
        def greet(row, carry):
            tell(barrier, row * Y_COUNT + y_at)
            return carry

        lax.fori_loop(1, RELAYED[0], greet, 0)
        lax.fori_loop(RELAYED[1], z_count, greet, 0)

    @pl.when(zero_double)
    def _():
        def greet(row, carry):
            tell(barrier, row * Y_COUNT)
            return carry

        lax.fori_loop(1, RELAYED[0], greet, 0)
        lax.fori_loop(RELAYED[1], z_count, greet, 0)

    @pl.when(late_member)
    def _():
        tell(barrier, HUB * Y_COUNT + y_at)

    greeted = jnp.where(early_target, recv_count, 0)
    greeted = jnp.where(z_at == HUB, z_count - EARLY_END, greeted)
    greeted = order + greeted + jnp.where(direct, 1, 0)

    @pl.when(greeted > 0)
    def _():
        pl.semaphore_wait(barrier, greeted)

    for step in range(1, Y_COUNT):

        @pl.when(order >= step)
        def _(step=step):
            tell(row_ready.at[step], z_at * Y_COUNT + lax.rem(y_at + Y_COUNT - step, Y_COUNT))

    @pl.when(early_target)
    def _():
        def answer(step, carry):
            tell(ready.at[step], ctx - step * Y_COUNT)
            return carry

        lax.fori_loop(1, recv_count + 1, answer, 0)

    @pl.when(direct)
    def _():
        tell(zero_ready.at[jnp.where(y_at == 0, 1, 0), z_at], jnp.maximum(y_at, 1))

    @pl.when(z_at == HUB)
    def _():
        for row in range(EARLY_END - 1, last):
            if row != HUB:
                tell(go, row * Y_COUNT + y_at)

    loads[0].wait()
    decay = decay_buf[...]
    loads[1].wait()
    loads[2].wait()
    product = key_buf[...].astype(F32) * value_buf[...].astype(F32)
    signal[0:64, :] = jnp.zeros((64, lane_count), F32)
    signal[64:, :] = product.astype(jnp.bfloat16).astype(F32)
    sub = lax.broadcasted_iota(jnp.int32, (ROWS, lane_count), 0).astype(F32)
    rate = [jnp.broadcast_to(decay_buf[r : r + 1, :], (ROWS, lane_count)) for r in range(mode_count)]
    leap = [jnp.exp(-float(ROWS) * rate[r]) for r in range(mode_count)]

    def gather(block, sums):
        rows = signal[pl.ds(pl.multiple_of(64 + ROWS * block, ROWS), ROWS), :]
        return tuple(leap[r] * sums[r] + rows for r in range(mode_count))

    sums = lax.fori_loop(
        0, block_count, gather, (jnp.zeros((ROWS, lane_count), F32),) * mode_count, unroll=4
    )
    for r in range(mode_count):
        fade = jnp.exp(-rate[r] * (float(ROWS - 1) - sub))
        own_state[r : r + 1, :] = jnp.sum(sums[r] * fade, axis=0, keepdims=True)

    def y_copy(step):
        peer_y = lax.rem(y_at + step, Y_COUNT)
        return pltpu.make_async_remote_copy(
            src_ref=own_state,
            dst_ref=row_states.at[step],
            send_sem=y_send.at[step],
            recv_sem=y_recv.at[step],
            device_id={"ctx": z_at * Y_COUNT + peer_y},
            device_id_type=MESH,
        )

    for step in range(1, Y_COUNT):

        @pl.when(order + step >= Y_COUNT)
        def _(step=step):
            y_copy(step).start()

    for step in range(1, Y_COUNT):

        @pl.when(order + step < Y_COUNT)
        def _(step=step):
            pl.semaphore_wait(row_ready.at[step], 1)
            y_copy(step).start()

    span = float(row_count)
    for step in range(1, z_count):
        power[step] = jnp.exp(decay * (-span * Y_COUNT * (step - 1)))
    def convolve():
        loads[3].wait()
        loads[4].wait()
        weight = weight_buf[...] * jnp.sqrt(2.0 * decay)
        weight_buf[...] = weight
        start = tuple(weight_buf[r : r + 1, :] * jnp.exp(-rate[r] * sub) for r in range(mode_count))

        def tabulate(block, modes):
            total = modes[0]
            for r in range(1, mode_count):
                total = total + modes[r]
            taps[pl.ds(pl.multiple_of(ROWS * block, ROWS), ROWS), :] = total
            for r in range(mode_count):
                table[block, r] = modes[r]
            return tuple(modes[r] * leap[r] for r in range(mode_count))

        lax.fori_loop(0, block_count, tabulate, start)

        for shift in range(ROWS):
            shifted[shift, 0:56, :] = jnp.zeros((56, lane_count), F32)
            shifted[shift, 56:, :] = signal[64 - shift : 64 + row_count - shift, :]
        gain = gain_buf[...]
        for group in range(row_count // 64):

            def slide(lag, sums, group=group):
                for shift in range(ROWS):
                    tap = taps[pl.ds(lag * ROWS + shift, 1), :]
                    rows = shifted[shift, pl.ds(pl.multiple_of(64 * group + 56 - ROWS * lag, ROWS), 64), :]
                    sums = sums + tap * rows
                return sums

            rows = slice(64 * group, 64 * group + 64)
            first = gain * signal[64 + 64 * group : 128 + 64 * group, :]
            base[rows, :] = lax.fori_loop(0, 8 * group + 8, slide, first)
        loads[5].wait()

    @pl.when(zero)
    def _():
        convolve()

    y_f = y_at.astype(F32)
    whole, ahead = [], []
    for step in range(Y_COUNT):
        source = lax.rem(y_at - step + Y_COUNT, Y_COUNT)
        whole.append(jnp.exp(decay * (-span * (Y_COUNT - 1 - source).astype(F32))))
        seen = jnp.where(source < y_at, 1.0, 0.0)
        gap = jnp.maximum(y_at - 1 - source, 0).astype(F32)
        ahead.append(seen * jnp.exp(decay * (-span * gap)))
    total = own_state[...] * whole[0]
    before = jnp.zeros_like(decay)
    for step in range(1, Y_COUNT):
        y_copy(step).wait_recv()
        total = total + row_states[step] * whole[step]
        before = before + row_states[step] * ahead[step]
    row_total[...] = total
    prefix[...] = before

    def z_copy(step):
        return pltpu.make_async_remote_copy(
            src_ref=row_total,
            dst_ref=column_states.at[step],
            send_sem=z_send.at[step],
            recv_sem=z_recv.at[step],
            device_id={"ctx": ctx + step * Y_COUNT},
            device_id_type=MESH,
        )

    def zero_copy(row, column):
        return pltpu.make_async_remote_copy(
            src_ref=row_total,
            dst_ref=zero_state,
            send_sem=zero_send.at[column, row],
            recv_sem=zero_recv,
            device_id={"ctx": row * Y_COUNT + (0 if column else y_at)},
            device_id_type=MESH,
        )

    def zero_arrive():
        zero_copy(z_at, 0).wait_recv()
        near[...] += power[z_at] * zero_state[...]

    def relay_copy(row):
        return pltpu.make_async_remote_copy(
            src_ref=zero_state,
            dst_ref=zero_state,
            send_sem=zero_send.at[0, row],
            recv_sem=zero_recv,
            device_id={"ctx": row * Y_COUNT + y_at},
            device_id_type=MESH,
        )

    def zero_visit(act):
        for row in NEAR + FAR:

            @pl.when(zero_sender)
            def _(row=row):
                act(row, 0)

            @pl.when(zero_double)
            def _(row=row):
                act(row, 1)

    def zero_start(row, column):
        pl.semaphore_wait(zero_ready.at[column, row], 1)
        zero_copy(row, column).start()

    @pl.when(jnp.logical_and(apart, zero))
    def _():
        zero_visit(zero_start)

    near[...] = jnp.zeros_like(decay)

    def arrive(step, carry):
        z_copy(step).wait_recv()
        near[...] += power[step] * column_states[step]
        return carry

    @pl.when(forwards)
    def _():
        lax.fori_loop(1, recv_count + 1, arrive, 0)
        row_total[...] += power[2] * near[...]

    @pl.when(jnp.logical_and(late_member, z_at < last))
    def _():
        pl.semaphore_wait(go, 1)

    @pl.when(early_sender)
    def _():
        def dispatch(step, carry):
            pl.semaphore_wait(ready.at[step], 1)
            z_copy(step).start()
            return carry

        lax.fori_loop(1, send_count + 1, dispatch, 0)

    @pl.when(jnp.logical_not(early_sender))
    def _():
        def dispatch(at, carry):
            z_copy(send_count - at).start()
            return carry

        lax.fori_loop(0, send_count, dispatch, 0)

    @pl.when(relays)
    def _():
        zero_arrive()
        for row in reversed(range(*RELAYED)):
            relay_copy(row).start()

    @pl.when(jnp.logical_not(zero))
    def _():
        convolve()

    @pl.when(jnp.logical_not(forwards))
    def _():
        lax.fori_loop(1, recv_count + 1, arrive, 0)

    @pl.when(jnp.logical_and(from_zero, jnp.logical_not(relays)))
    def _():
        zero_arrive()

    entering = prefix[...] + near[...] * jnp.exp(decay * (-span * y_f))
    near[...] = entering * jnp.exp(-decay)
    modes = [jnp.broadcast_to(near[r : r + 1, :], (ROWS, lane_count)) for r in range(mode_count)]

    def finish(pair, carry):
        tiles = []
        for half in range(2):
            block = 2 * pair + half
            terms = [table[block, r] * modes[r] for r in range(mode_count)]
            terms.append(base[pl.ds(pl.multiple_of(ROWS * block, ROWS), ROWS), :])
            while len(terms) > 1:
                terms = [sum(terms[at : at + 2][1:], terms[at]) for at in range(0, len(terms), 2)]
            tiles.append(terms[0])
        rows = pl.ds(pl.multiple_of(2 * ROWS * pair, 2 * ROWS), 2 * ROWS)
        mixed = query_buf[rows, :].astype(F32) * jnp.concatenate(tiles, axis=0)
        out_buf[rows, :] = mixed.astype(jnp.bfloat16)
        return carry

    lax.fori_loop(0, block_count // 2, finish, 0, unroll=2)
    store = pltpu.make_async_copy(out_buf, out_hbm, store_sem)
    store.start()
    for step in range(1, Y_COUNT):
        y_copy(step).wait_send()

    def drain(step, carry):
        z_copy(step).wait_send()
        return carry

    lax.fori_loop(1, send_count + 1, drain, 0)

    @pl.when(jnp.logical_and(apart, zero))
    def _():
        zero_visit(lambda row, column: zero_copy(row, column).wait_send())

    @pl.when(relays)
    def _():
        for row in range(*RELAYED):
            relay_copy(row).wait_send()

    store.wait()


def local(query_proj, key_proj, value_proj, decays, residues, skip_gain):
    row_count, lane_count = query_proj.shape
    mode_count = decays.shape[1]
    ctx_count = lax.axis_size("ctx")
    z_count = ctx_count // Y_COUNT
    state = (mode_count, lane_count)
    wide = (row_count, lane_count)
    block_count = row_count // ROWS
    any_space = pl.BlockSpec(memory_space=pl.ANY)
    return pl.pallas_call(
        kernel,
        out_shape=jax.ShapeDtypeStruct(wide, jnp.bfloat16),
        in_specs=[any_space] * 6,
        out_specs=any_space,
        scratch_shapes=[
            pltpu.VMEM(wide, jnp.bfloat16),
            pltpu.VMEM(wide, jnp.bfloat16),
            pltpu.VMEM(wide, jnp.bfloat16),
            pltpu.VMEM(state, F32),
            pltpu.VMEM(state, F32),
            pltpu.VMEM((1, lane_count), F32),
            pltpu.VMEM(wide, jnp.bfloat16),
            pltpu.VMEM((64 + row_count, lane_count), F32),
            pltpu.VMEM((ROWS, 56 + row_count, lane_count), F32),
            pltpu.VMEM((block_count, mode_count, ROWS, lane_count), F32),
            pltpu.VMEM(wide, F32),
            pltpu.VMEM(wide, F32),
            pltpu.VMEM(state, F32),
            pltpu.VMEM((z_count,) + state, F32),
            pltpu.VMEM(state, F32),
            pltpu.VMEM(state, F32),
            pltpu.VMEM((Y_COUNT,) + state, F32),
            pltpu.VMEM(state, F32),
            pltpu.VMEM((z_count,) + state, F32),
            pltpu.VMEM(state, F32),
            pltpu.SemaphoreType.DMA((6,)),
            pltpu.SemaphoreType.DMA,
            pltpu.SemaphoreType.DMA((Y_COUNT,)),
            pltpu.SemaphoreType.DMA((Y_COUNT,)),
            pltpu.SemaphoreType.DMA((z_count,)),
            pltpu.SemaphoreType.DMA((z_count,)),
            pltpu.SemaphoreType.REGULAR((Y_COUNT,)),
            pltpu.SemaphoreType.REGULAR((EARLY_END,)),
            pltpu.SemaphoreType.REGULAR,
            pltpu.SemaphoreType.DMA((2, z_count)),
            pltpu.SemaphoreType.DMA,
            pltpu.SemaphoreType.REGULAR((2, z_count)),
        ],
        compiler_params=pltpu.CompilerParams(collective_id=0, has_side_effects=True),
    )(query_proj, key_proj, value_proj, decays.T, residues.T, skip_gain.reshape(1, lane_count))


def solution(mesh):
    return jax.shard_map(
        local,
        mesh=mesh,
        in_specs=(P("ctx", "ch"), P("ctx", "ch"), P("ctx", "ch"), P(), P(), P("ch")),
        out_specs=P("ctx", "ch"),
        check_vma=False,
    )
```
